512 devices in a mesh: row: 16 (over x, y), col: 32 (over z, core).
Axes of the slice: x: 4, y: 4, z: 16, core: 2. Of those that a mesh axis runs over, the one named last changes fastest.
Arguments:
- rhs: float32 [36864, 128], P('row'), may hold values from -6 to 6
- factor: float32 [34816, 4096], P('row', 'col'), may hold values from -0.09375 to 0.09375
- inverses: float32 [2, 2048, 2048], P(None, 'col', 'row'), may hold values from -1 to 3, as said below
Outputs:
- solution: float32 [4096, 128], P('col')
- remaining: float32 [32768, 128], P('row')
The draws below stay inside these ranges and needn't reach their ends.
Inputs may be any that keep to these rules, and one draw needn't show every extreme that they name: Each inverses[k] is lower triangular in panel order with positive diagonal entries.
All inputs are finite; a program needn't handle non-finite values.
Results may differ from the reference program's by a relative error of at most 0.000068.
Values sent between devices are 32-bit elements; how exact they have to be, the bound alone decides.
No kernel may reach another device: no remote copies, remote signals or barrier semaphores. Data moves between devices by JAX's collectives and lax.ppermute only.
A program may use at most 64 MiB of HBM per device.

```python
import math
import jax
import jax.numpy as jnp
from jax import lax

PANEL = 2048
DENSITIES = 128
TRAIL_DEV = 2048
BLOCK_ROW = 128
BLOCK_COL = 64
TRAIL = 32768
N_ROW = 16
N_COL = 32


def draw_inverses(key, part):
    key_low, key_diag = jax.random.split(jax.random.fold_in(key, 17))
    lower = jax.random.truncated_normal(key_low, -4.0, 4.0, (2, PANEL, PANEL), jnp.float32) * (1.5 / math.sqrt(PANEL))
    diagonal = jax.random.uniform(key_diag, (2, PANEL), jnp.float32, 0.5, 1.5)
    return jnp.tril(lower, -1) + diagonal[:, :, None] * jnp.eye(PANEL, dtype=jnp.float32)


def shard_levels(rng, dims, cuts, smallest, largest):
    gain, own = 1.0, jax.random.fold_in(rng, 6)
    for position, shards_of in cuts:
        steps = jnp.exp(jax.random.uniform(jax.random.fold_in(own, position), (shards_of,), jnp.float32, smallest / len(cuts), largest / len(cuts)))
        gain = gain * jnp.repeat(steps, dims[position] // shards_of).reshape([-1 if axis == position else 1 for axis in range(len(dims))])
    return gain


def bell_draw(stream_key, dims, deviation, bound, pieces=(), kind=jnp.bfloat16):
    level = shard_levels(stream_key, dims, pieces, -0.22, 0.18) if pieces else 1.0
    drawn = jax.random.normal(stream_key, dims, jnp.float32) * deviation * level
    return jnp.minimum(jnp.maximum(drawn, -bound), bound).astype(kind)


def setup_inputs(seed: int = 0) -> dict:
    arg_keys = jax.random.split(jax.random.key(seed), 4)
    return {
        "rhs": bell_draw(arg_keys[0], (2 * PANEL + TRAIL, DENSITIES), 1.0, 6.0, ((0, 16),), jnp.float32),
        "factor": bell_draw(arg_keys[1], (PANEL + TRAIL, 2 * PANEL), (2 * PANEL) ** -0.5, 0.09375, ((0, 16), (1, 32)), jnp.float32),
        "inverses": draw_inverses(jax.random.fold_in(arg_keys[3], 71), 0),
    }


def product(left, right):
    return jnp.dot(left, right, precision=lax.Precision.HIGHEST, preferred_element_type=jnp.float32)


def reference(rhs, factor, inverses):
    rhs_blocks = rhs.reshape(N_ROW, 2 * BLOCK_ROW + TRAIL_DEV, DENSITIES)
    first_rhs = rhs_blocks[:, :BLOCK_ROW].reshape(PANEL, DENSITIES)
    second_rhs = rhs_blocks[:, BLOCK_ROW:2 * BLOCK_ROW].reshape(PANEL, DENSITIES)
    trailing = rhs_blocks[:, 2 * BLOCK_ROW:].reshape(TRAIL, DENSITIES)
    factor_blocks = factor.reshape(N_ROW, BLOCK_ROW + TRAIL_DEV, N_COL, 2, BLOCK_COL)
    first_cols = factor_blocks[:, :, :, 0, :].reshape(N_ROW, BLOCK_ROW + TRAIL_DEV, PANEL)
    second_cols = factor_blocks[:, :, :, 1, :].reshape(N_ROW, BLOCK_ROW + TRAIL_DEV, PANEL)
    coupling = first_cols[:, :BLOCK_ROW].reshape(PANEL, PANEL)
    trail_first = first_cols[:, BLOCK_ROW:].reshape(TRAIL, PANEL)
    trail_second = second_cols[:, BLOCK_ROW:].reshape(TRAIL, PANEL)
    first_sol = product(inverses[0], first_rhs)
    reduced = second_rhs - product(coupling, first_sol)
    second_sol = product(inverses[1], reduced)
    remaining = trailing - product(trail_first, first_sol) - product(trail_second, second_sol)
    solution = jnp.stack([first_sol.reshape(N_COL, BLOCK_COL, DENSITIES), second_sol.reshape(N_COL, BLOCK_COL, DENSITIES)], 1)
    return solution.reshape(2 * PANEL, DENSITIES), remaining
```

```python
import jax
import jax.numpy as jnp
from jax import lax
from jax.sharding import Mesh
from jax.sharding import PartitionSpec as P

ROW = ("x", "y")
COL = ("z", "core")


def exchanged(blocks, axis):
    return lax.all_to_all(blocks, axis, split_axis=0, concat_axis=0, tiled=True)


def from_everyone(array, axis):
    return exchanged(jnp.broadcast_to(array, (lax.axis_size(axis), *array.shape)), axis)


def taken_together(array, axis):
    return jnp.sum(from_everyone(array, axis), axis=0)


def my_sum(array, axis):
    count = lax.axis_size(axis)
    blocks = array.reshape(count, array.shape[0] // count, *array.shape[1:])
    return jnp.sum(exchanged(blocks, axis), axis=0)


def gathered(array, axis):
    blocks = from_everyone(array, axis)
    return blocks.reshape(-1, *array.shape[1:])


def product(left, right):
    return jnp.dot(left, right, precision=lax.Precision.HIGHEST, preferred_element_type=jnp.float32)


def local(rhs, factor, inverses):
    span_rows = inverses.shape[2]
    span_cols = factor.shape[1] // 2
    first_rhs = rhs[:span_rows]
    second_rhs = rhs[span_rows : 2 * span_rows]
    trailing = rhs[2 * span_rows :]
    first_sol = taken_together(product(inverses[0], first_rhs), ROW)
    coupled = gathered(my_sum(product(factor[:span_rows, :span_cols], first_sol), COL), COL)
    carried = product(factor[span_rows:, :span_cols], first_sol)
    second_sol = taken_together(product(inverses[1], second_rhs - coupled), ROW)
    terms = carried + product(factor[span_rows:, span_cols:], second_sol)
    terms = my_sum(my_sum(terms, "core"), "z")
    rows = terms.shape[0]
    start = (lax.axis_index("core") * lax.axis_size("z") + lax.axis_index("z")) * rows
    mine = lax.dynamic_slice_in_dim(trailing, start, rows) - terms
    remaining = gathered(gathered(mine, "z"), "core")
    return (jnp.concatenate([first_sol, second_sol], 0), remaining)


def solution(mesh):
    rows, cols = mesh.devices.shape
    shape = (4, rows // 4, cols // 2, 2)
    torus = Mesh(mesh.devices.reshape(shape), (*ROW, *COL))
    in_specs = (P(ROW, None), P(ROW, COL), P(None, COL, ROW))
    out_specs = (P(COL, None), P(ROW, None))
    return jax.shard_map(local, mesh=torus, in_specs=in_specs, out_specs=out_specs, check_vma=False)
```

```python
import jax
import jax.numpy as jnp
from jax import lax
from jax.sharding import Mesh
from jax.sharding import PartitionSpec as P

ROW = ("x", "y")
COL = ("z", "core")


def exchanged(blocks, axis):
    return lax.all_to_all(blocks, axis, split_axis=0, concat_axis=0, tiled=True)


def from_everyone(array, axis):
    return exchanged(jnp.broadcast_to(array, (lax.axis_size(axis), *array.shape)), axis)


def taken_together(array, axis):
    return jnp.sum(from_everyone(array, axis), axis=0)


def my_sum(array, axis):
    count = lax.axis_size(axis)
    blocks = array.reshape(count, array.shape[0] // count, *array.shape[1:])
    return jnp.sum(exchanged(blocks, axis), axis=0)


def gathered(array, axis):
    blocks = from_everyone(array, axis)
    return blocks.reshape(-1, *array.shape[1:])


def product(left, right):
    return jnp.dot(left, right, precision=lax.Precision.HIGHEST, preferred_element_type=jnp.float32)


def local(rhs, factor, inverses):
    span_rows = inverses.shape[2]
    span_cols = factor.shape[1] // 2
    first_rhs = rhs[:span_rows]
    second_rhs = rhs[span_rows : 2 * span_rows]
    rows = (rhs.shape[0] - 2 * span_rows) // (lax.axis_size("z") * lax.axis_size("core"))
    place = lax.axis_index("core") * lax.axis_size("z") + lax.axis_index("z")
    trailing = lax.dynamic_slice_in_dim(rhs, 2 * span_rows + place * rows, rows)
    first_part = product(inverses[0], first_rhs)
    coupling = factor[:span_rows, :span_cols]
    first_part, trailing, second_rhs, second_inverse, coupling = lax.optimization_barrier(
        (first_part, trailing, second_rhs, inverses[1], coupling)
    )
    first_sol = taken_together(first_part, ROW)
    coupled = gathered(my_sum(product(coupling, first_sol), COL), COL)
    second_sol = taken_together(product(second_inverse, second_rhs - coupled), ROW)
    both = jnp.concatenate([first_sol, second_sol], 0)
    both, terms = lax.optimization_barrier((both, product(factor[span_rows:], both)))
    terms = my_sum(my_sum(terms, "core"), "z")
    remaining = gathered(gathered(trailing - terms, "z"), "core")
    both, remaining = lax.optimization_barrier((both, remaining))
    return (both, remaining)


def solution(mesh):
    rows, cols = mesh.devices.shape
    shape = (4, rows // 4, cols // 2, 2)
    torus = Mesh(mesh.devices.reshape(shape), (*ROW, *COL))
    in_specs = (P(ROW, None), P(ROW, COL), P(None, COL, ROW))
    out_specs = (P(COL, None), P(ROW, None))
    return jax.shard_map(local, mesh=torus, in_specs=in_specs, out_specs=out_specs, check_vma=False)
```

```python
import jax
import jax.numpy as jnp
from jax import lax
from jax.sharding import Mesh
from jax.sharding import PartitionSpec as P

ROW = ("x", "y")
NEAR = ("zb", "zc", "core")
FAR = "za"
PARITY = ("za", "zb")
Z = ("za", "zb", "zc")
COL = (*Z, "core")
SWAP = [(0, 1), (1, 0)]


def exchanged(blocks, axis):
    return lax.all_to_all(blocks, axis, split_axis=0, concat_axis=0, tiled=True)


def from_everyone(array, axis):
    return exchanged(jnp.broadcast_to(array, (lax.axis_size(axis), *array.shape)), axis)


def taken_together(array, axis):
    return jnp.sum(from_everyone(array, axis), axis=0)


def my_sum(array, axis):
    count = lax.axis_size(axis)
    blocks = array.reshape(count, array.shape[0] // count, *array.shape[1:])
    return jnp.sum(exchanged(blocks, axis), axis=0)


def gathered(array, axis):
    return from_everyone(array, axis).reshape(-1, *array.shape[1:])


def product(left, right):
    return jnp.dot(left, right, precision=lax.Precision.HIGHEST, preferred_element_type=jnp.float32)


def part_of(array, start, rows):
    return lax.dynamic_slice(array, (start, jnp.uint32(0)), (rows, array.shape[1]))


def local(rhs, factor, inverses):
    span_rows = inverses.shape[2]
    span_cols = factor.shape[1] // 2
    first_rhs = rhs[:span_rows]
    second_rhs = rhs[span_rows : 2 * span_rows]
    spots = lax.axis_size(Z)
    rows = (rhs.shape[0] - 2 * span_rows) // (2 * spots)
    half = spots * rows
    core = lax.axis_index("core").astype(jnp.uint32)
    mine_at, other_at = core * half, (1 - core) * half
    place = 2 * span_rows + mine_at + lax.axis_index(Z).astype(jnp.uint32) * rows
    first_part = product(inverses[0], first_rhs)
    first_part, second_rhs, mine_at, other_at, place = lax.optimization_barrier(
        (first_part, second_rhs, mine_at, other_at, place)
    )

    first_sol = taken_together(first_part, ROW)
    coupled = lax.optimization_barrier(product(factor[:span_rows, :span_cols], first_sol))
    coupled = gathered(taken_together(my_sum(coupled, NEAR), FAR), NEAR)
    second_sol = taken_together(product(inverses[1], second_rhs - coupled), ROW)

    terms = product(factor[span_rows:], jnp.concatenate([first_sol, second_sol], 0))
    terms = terms.reshape(2, spots // 2, 2, rows, -1).swapaxes(1, 2).reshape(2 * half, -1)
    sent = part_of(terms, other_at, half)
    kept = part_of(terms, mine_at, half)
    sent, kept, first_sol, second_sol, rhs = lax.optimization_barrier((sent, kept, first_sol, second_sol, rhs))
    taken = lax.ppermute(sent, "core", SWAP)
    both = jnp.concatenate([first_sol, second_sol], 0)
    trailing = part_of(rhs, place, rows)
    taken, both, trailing = lax.optimization_barrier((taken, both, trailing))
    terms = my_sum(my_sum(kept + taken, "zc"), PARITY)

    mine = lax.all_gather(trailing - terms, Z, axis=0, tiled=True)
    other = lax.ppermute(mine, "core", SWAP)
    remaining = jnp.concatenate([mine, mine], 0)
    remaining = lax.dynamic_update_slice(remaining, other, (other_at, jnp.uint32(0)))
    return (both, remaining)


def solution(mesh):
    rows, cols = mesh.devices.shape
    shape = (4, rows // 4, cols // 8, 2, 2, 2)
    torus = Mesh(mesh.devices.reshape(shape), (*ROW, *COL))
    in_specs = (P(ROW, None), P(ROW, COL), P(None, COL, ROW))
    out_specs = (P(COL, None), P(ROW, None))
    return jax.shard_map(local, mesh=torus, in_specs=in_specs, out_specs=out_specs, check_vma=False)
```

```python
import jax
import jax.numpy as jnp
from jax import lax
from jax.sharding import Mesh
from jax.sharding import PartitionSpec as P

ROW = ("x", "y")
NEAR = ("pair", "core")
Z = ("parity", "pair")
COL = (*Z, "core")
SWAP = [(0, 1), (1, 0)]


def exchanged(blocks, axis):
    return lax.all_to_all(blocks, axis, split_axis=0, concat_axis=0, tiled=True)


def from_everyone(array, axis):
    return exchanged(jnp.broadcast_to(array, (lax.axis_size(axis), *array.shape)), axis)


def taken_together(array, axis):
    return jnp.sum(from_everyone(array, axis), axis=0)


def my_sum(array, axis):
    count = lax.axis_size(axis)
    blocks = array.reshape(count, array.shape[0] // count, *array.shape[1:])
    return jnp.sum(exchanged(blocks, axis), axis=0)


def gathered(array, axis):
    return from_everyone(array, axis).reshape(-1, *array.shape[1:])


def product(left, right):
    return jnp.dot(left, right, precision=lax.Precision.HIGHEST, preferred_element_type=jnp.float32)


def part_of(array, start, rows):
    return lax.dynamic_slice(array, (start, jnp.uint32(0)), (rows, array.shape[1]))


def local(rhs, factor, inverses):
    span_rows = inverses.shape[2]
    span_cols = factor.shape[1] // 2
    first_rhs = rhs[:span_rows]
    second_rhs = rhs[span_rows : 2 * span_rows]
    spots = lax.axis_size(Z)
    rows = (rhs.shape[0] - 2 * span_rows) // (2 * spots)
    half = spots * rows
    core = lax.axis_index("core").astype(jnp.uint32)
    pair = lax.axis_index("pair").astype(jnp.uint32)
    quarter = half // 2
    place = 2 * span_rows + core * half + lax.axis_index(Z).astype(jnp.uint32) * rows
    starts = (core * half, (1 - core) * half, pair * quarter, (1 - pair) * quarter, place)
    first_part = product(inverses[0], first_rhs)
    first_part, second_rhs, starts = lax.optimization_barrier((first_part, second_rhs, starts))
    half_kept, half_sent, quarter_kept, quarter_sent, place = starts

    first_sol = taken_together(first_part, ROW)
    coupled = lax.optimization_barrier(product(factor[:span_rows, :span_cols], first_sol))
    coupled = gathered(taken_together(my_sum(coupled, NEAR), "parity"), NEAR)
    second_sol = taken_together(product(inverses[1], second_rhs - coupled), ROW)

    both = lax.optimization_barrier(jnp.concatenate([first_sol, second_sol], 0))
    terms = product(factor[span_rows:], both)
    terms = terms.reshape(2, spots // 2, 2, rows, -1).swapaxes(1, 2).reshape(2 * half, -1)
    sent, kept = part_of(terms, half_sent, half), part_of(terms, half_kept, half)
    sent, kept, rhs = lax.optimization_barrier((sent, kept, rhs))
    taken = lax.ppermute(sent, "core", SWAP)
    trailing = part_of(rhs, place, rows)
    taken, trailing = lax.optimization_barrier((taken, trailing))
    terms = kept + taken
    sent, kept = part_of(terms, quarter_sent, quarter), part_of(terms, quarter_kept, quarter)
    terms = my_sum(kept + lax.ppermute(sent, "pair", SWAP), "parity")

    mine = lax.all_gather(trailing - terms, Z, axis=0, tiled=True)
    other = lax.ppermute(mine, "core", SWAP)
    remaining = jnp.where(
        lax.axis_index("core") == 0, jnp.concatenate([mine, other], 0), jnp.concatenate([other, mine], 0)
    )
    return (both, remaining)


def solution(mesh):
    rows, cols = mesh.devices.shape
    shape = (4, rows // 4, cols // 4, 2, 2)
    torus = Mesh(mesh.devices.reshape(shape), (*ROW, *COL))
    in_specs = (P(ROW, None), P(ROW, COL), P(None, COL, ROW))
    out_specs = (P(COL, None), P(ROW, None))
    return jax.shard_map(local, mesh=torus, in_specs=in_specs, out_specs=out_specs, check_vma=False)
```

```python
import jax
import jax.numpy as jnp
from jax import lax
from jax.sharding import Mesh
from jax.sharding import PartitionSpec as P

ROW = ("x", "y")
NEAR = ("pair", "core")
Z = ("parity", "pair")
COL = (*Z, "core")
SWAP = [(0, 1), (1, 0)]


def exchanged(blocks, axis):
    return lax.all_to_all(blocks, axis, split_axis=0, concat_axis=0, tiled=True)


def from_everyone(array, axis):
    return exchanged(jnp.broadcast_to(array, (lax.axis_size(axis), *array.shape)), axis)


def taken_together(array, axis):
    return jnp.sum(from_everyone(array, axis), axis=0)


def my_sum(array, axis):
    count = lax.axis_size(axis)
    blocks = array.reshape(count, array.shape[0] // count, *array.shape[1:])
    return jnp.sum(exchanged(blocks, axis), axis=0)


def gathered(array, axis):
    return from_everyone(array, axis).reshape(-1, *array.shape[1:])


def product(left, right):
    return jnp.dot(left, right, precision=lax.Precision.HIGHEST, preferred_element_type=jnp.float32)


def part_of(array, start, rows):
    return lax.dynamic_slice(array, (start, 0), (rows, array.shape[1]), allow_negative_indices=False)


def every_other(blocks, first, which):
    sizes = (blocks.shape[0] - 1, 1, *blocks.shape[2:])
    part = lax.dynamic_slice(blocks, (first, which, 0, 0), sizes, allow_negative_indices=False)
    return part.reshape(-1, blocks.shape[-1])


def local(rhs, factor, inverses):
    span_rows = inverses.shape[2]
    span_cols = factor.shape[1] // 2
    first_rhs = rhs[:span_rows]
    second_rhs = rhs[span_rows : 2 * span_rows]
    spots = lax.axis_size(Z)
    rows = (rhs.shape[0] - 2 * span_rows) // (2 * spots)
    half = spots * rows // 2
    core = lax.axis_index("core")
    pair = lax.axis_index("pair")
    place = 2 * span_rows + (core * spots + lax.axis_index(Z)) * rows
    starts = (core * half, (1 - core) * half, pair, 1 - pair, place, jnp.int32(1))
    first_part = product(inverses[0], first_rhs)
    first_part, second_rhs, starts = lax.optimization_barrier((first_part, second_rhs, starts))
    half_kept, half_sent, pair, other_pair, place, one = starts

    first_sol = taken_together(first_part, ROW)
    coupled = lax.optimization_barrier(product(factor[:span_rows, :span_cols], first_sol))
    coupled = my_sum(coupled, NEAR)
    coupled, factor = lax.optimization_barrier((coupled, factor))
    blocks = factor.reshape(-1, 2, span_rows // 2, factor.shape[1])
    kept, sent = every_other(blocks, one, pair), every_other(blocks, one, other_pair)
    sent, kept, coupled = lax.optimization_barrier((sent, kept, coupled))
    came = lax.ppermute(sent, "pair", SWAP)
    coupled = gathered(taken_together(coupled, "parity"), NEAR)
    came, coupled = lax.optimization_barrier((came, coupled))
    second_part = product(inverses[1], second_rhs - coupled)
    second_sol = taken_together(second_part, ROW)

    both = lax.optimization_barrier(jnp.concatenate([first_sol, second_sol], 0))
    theirs = lax.ppermute(both, "pair", SWAP)
    terms = product(kept, both)
    theirs, terms = lax.optimization_barrier((theirs, terms))
    terms = terms + product(came, theirs)
    sent, kept = part_of(terms, half_sent, half), part_of(terms, half_kept, half)
    sent, kept, rhs = lax.optimization_barrier((sent, kept, rhs))
    taken = lax.ppermute(sent, "core", SWAP)
    trailing = part_of(rhs, place, rows)
    taken, trailing = lax.optimization_barrier((taken, trailing))
    terms = my_sum(kept + taken, "parity")

    mine = lax.all_gather(trailing - terms, Z, axis=0, tiled=True)
    other = lax.ppermute(mine, "core", SWAP)
    remaining = jnp.where(
        lax.axis_index("core") == 0, jnp.concatenate([mine, other], 0), jnp.concatenate([other, mine], 0)
    )
    return (both, remaining)


def solution(mesh):
    rows, cols = mesh.devices.shape
    shape = (4, rows // 4, cols // 4, 2, 2)
    torus = Mesh(mesh.devices.reshape(shape), (*ROW, *COL))
    in_specs = (P(ROW, None), P(ROW, COL), P(None, COL, ROW))
    out_specs = (P(COL, None), P(ROW, None))
    return jax.shard_map(local, mesh=torus, in_specs=in_specs, out_specs=out_specs, check_vma=False)
```

```python
import jax
import jax.numpy as jnp
from jax import lax
from jax.experimental.layout import Layout, with_layout_constraint
from jax.sharding import Mesh
from jax.sharding import PartitionSpec as P

ROW = ("x", "y")
NEAR = ("pair", "core")
Z = ("parity", "pair")
COL = (*Z, "core")
SWAP = [(0, 1), (1, 0)]


def exchanged(blocks, axis):
    return lax.all_to_all(blocks, axis, split_axis=0, concat_axis=0, tiled=True)


def from_everyone(array, axis):
    return exchanged(jnp.broadcast_to(array, (lax.axis_size(axis), *array.shape)), axis)


def taken_together(array, axis):
    return jnp.sum(from_everyone(array, axis), axis=0)


def my_sum(array, axis):
    count = lax.axis_size(axis)
    blocks = array.reshape(count, array.shape[0] // count, *array.shape[1:])
    return jnp.sum(exchanged(blocks, axis), axis=0)


def product(left, right):
    return jnp.dot(left, right, precision=lax.Precision.HIGHEST, preferred_element_type=jnp.float32)


def part_of(array, start, rows):
    return lax.dynamic_slice(array, (start, 0), (rows, array.shape[1]), allow_negative_indices=False)


def local(rhs, factor, inverses):
    span_rows = inverses.shape[2]
    span_cols = factor.shape[1] // 2
    first_rhs = rhs[:span_rows]
    second_rhs = rhs[span_rows : 2 * span_rows]
    spots = lax.axis_size(Z)
    rows = (rhs.shape[0] - 2 * span_rows) // (2 * spots)
    half = spots * rows
    core = lax.axis_index("core")
    pair = lax.axis_index("pair")
    quarter = half // 2
    place = 2 * span_rows + core * half + lax.axis_index(Z) * rows
    near_rows = span_rows // lax.axis_size(NEAR)
    near = lax.axis_index(NEAR) * near_rows
    starts = (core * half, (1 - core) * half, pair * quarter, (1 - pair) * quarter, near, place)
    first_part = product(inverses[0], first_rhs)
    first_part, second_rhs, starts = lax.optimization_barrier((first_part, second_rhs, starts))
    half_kept, half_sent, quarter_kept, quarter_sent, near, place = starts

    first_sol = taken_together(first_part, ROW)
    coupled = lax.optimization_barrier(product(factor[:span_rows, :span_cols], first_sol))
    coupled = with_layout_constraint(coupled, Layout((0, 1)))
    coupled = lax.all_gather(coupled, NEAR, axis=0)
    coupled = lax.dynamic_slice(
        coupled, (0, near, 0), (coupled.shape[0], near_rows, coupled.shape[2]), allow_negative_indices=False
    )
    coupled = taken_together(jnp.sum(coupled, axis=0), "parity")
    coupled = lax.all_gather(coupled, NEAR, axis=0, tiled=True)
    second_sol = taken_together(product(inverses[1], second_rhs - coupled), ROW)

    both = lax.optimization_barrier(jnp.concatenate([first_sol, second_sol], 0))
    terms = with_layout_constraint(product(factor[span_rows:], both), Layout((0, 1)))
    terms = terms.reshape(2, spots // 2, 2, rows, -1).swapaxes(1, 2).reshape(2 * half, -1)
    sent, kept = part_of(terms, half_sent, half), part_of(terms, half_kept, half)
    sent, kept, rhs = lax.optimization_barrier((sent, kept, rhs))
    taken = lax.ppermute(sent, "core", SWAP)
    trailing = part_of(rhs, place, rows)
    taken, trailing = lax.optimization_barrier((taken, trailing))
    terms = kept + taken
    sent, kept = part_of(terms, quarter_sent, quarter), part_of(terms, quarter_kept, quarter)
    taken = part_of(lax.all_gather(sent, "pair", axis=0, tiled=True), quarter_sent, quarter)
    terms = my_sum(kept + taken, "parity")

    mine = lax.all_gather(trailing - terms, Z, axis=0, tiled=True)
    other = lax.ppermute(mine, "core", SWAP)
    remaining = jnp.where(
        lax.axis_index("core") == 0, jnp.concatenate([mine, other], 0), jnp.concatenate([other, mine], 0)
    )
    return (both, remaining)


def solution(mesh):
    rows, cols = mesh.devices.shape
    shape = (4, rows // 4, cols // 4, 2, 2)
    torus = Mesh(mesh.devices.reshape(shape), (*ROW, *COL))
    in_specs = (P(ROW, None), P(ROW, COL), P(None, COL, ROW))
    out_specs = (P(COL, None), P(ROW, None))
    return jax.shard_map(local, mesh=torus, in_specs=in_specs, out_specs=out_specs, check_vma=False)
```

```python
import jax
import jax.numpy as jnp
from jax import lax
from jax.experimental.layout import Layout, with_layout_constraint
from jax.sharding import Mesh
from jax.sharding import PartitionSpec as P

ROW = ("x", "y")
NEAR = ("pair", "core")
Z = ("parity", "pair")
COL = (*Z, "core")
SWAP = [(0, 1), (1, 0)]
CROSSED = [[0, 3], [1, 2]]


def exchanged(blocks, axis):
    return lax.all_to_all(blocks, axis, split_axis=0, concat_axis=0, tiled=True)


def from_everyone(array, axis):
    return exchanged(jnp.broadcast_to(array, (lax.axis_size(axis), *array.shape)), axis)


def taken_together(array, axis):
    return jnp.sum(from_everyone(array, axis), axis=0)


def my_sum(array, axis):
    count = lax.axis_size(axis)
    blocks = array.reshape(count, array.shape[0] // count, *array.shape[1:])
    return jnp.sum(exchanged(blocks, axis), axis=0)


def product(left, right):
    return jnp.dot(left, right, precision=lax.Precision.HIGHEST, preferred_element_type=jnp.float32)


def part_of(array, start, rows):
    return lax.dynamic_slice(array, (start, 0), (rows, array.shape[1]), allow_negative_indices=False)


def local(rhs, factor, inverses):
    span_rows = inverses.shape[2]
    span_cols = factor.shape[1] // 2
    first_rhs = rhs[:span_rows]
    second_rhs = rhs[span_rows : 2 * span_rows]
    spots = lax.axis_size(Z)
    rows = (rhs.shape[0] - 2 * span_rows) // (2 * spots)
    half = spots * rows
    side = lax.axis_index("core") ^ lax.axis_index("pair")
    pair = lax.axis_index("pair")
    quarter = half // 2
    place = 2 * span_rows + side * half + lax.axis_index(Z) * rows
    near_rows = span_rows // lax.axis_size(NEAR)
    near = lax.axis_index(NEAR) * near_rows
    starts = (side * half, (1 - side) * half, pair * quarter, (1 - pair) * quarter, near, place)
    first_part = product(inverses[0], first_rhs)
    first_part, second_rhs, starts = lax.optimization_barrier((first_part, second_rhs, starts))
    half_kept, half_sent, quarter_kept, quarter_sent, near, place = starts

    first_sol = taken_together(first_part, ROW)
    coupled = lax.optimization_barrier(product(factor[:span_rows, :span_cols], first_sol))
    coupled = with_layout_constraint(coupled, Layout((0, 1)))
    coupled = lax.all_gather(coupled, NEAR, axis=0)
    coupled = lax.dynamic_slice(
        coupled, (0, near, 0), (coupled.shape[0], near_rows, coupled.shape[2]), allow_negative_indices=False
    )
    coupled = taken_together(jnp.sum(coupled, axis=0), "parity")
    coupled = lax.all_gather(coupled, NEAR, axis=0, tiled=True)
    second_sol = taken_together(product(inverses[1], second_rhs - coupled), ROW)

    both = lax.optimization_barrier(jnp.concatenate([first_sol, second_sol], 0))
    terms = with_layout_constraint(product(factor[span_rows:], both), Layout((0, 1)))
    terms = terms.reshape(2, spots // 2, 2, rows, -1).swapaxes(1, 2).reshape(2 * half, -1)
    sent, kept = part_of(terms, half_sent, half), part_of(terms, half_kept, half)
    sent, kept, rhs = lax.optimization_barrier((sent, kept, rhs))
    taken = lax.ppermute(sent, "core", SWAP)
    trailing = part_of(rhs, place, rows)
    taken, trailing = lax.optimization_barrier((taken, trailing))
    terms = kept + taken
    sent, kept = part_of(terms, quarter_sent, quarter), part_of(terms, quarter_kept, quarter)
    sent = lax.all_gather(sent, NEAR, axis=0, tiled=True, axis_index_groups=CROSSED)
    taken = part_of(sent, quarter_sent, quarter)
    terms = my_sum(kept + taken, "parity")

    rings = [[2 * z + (z + start) % 2 for z in range(spots)] for start in range(2)]
    mine = lax.all_gather(trailing - terms, COL, axis=0, tiled=True, axis_index_groups=rings)
    other = lax.ppermute(mine, "core", SWAP)
    remaining = jnp.where(
        side == 0, jnp.concatenate([mine, other], 0), jnp.concatenate([other, mine], 0)
    )
    return (both, remaining)


def solution(mesh):
    rows, cols = mesh.devices.shape
    shape = (4, rows // 4, cols // 4, 2, 2)
    torus = Mesh(mesh.devices.reshape(shape), (*ROW, *COL))
    in_specs = (P(ROW, None), P(ROW, COL), P(None, COL, ROW))
    out_specs = (P(COL, None), P(ROW, None))
    return jax.shard_map(local, mesh=torus, in_specs=in_specs, out_specs=out_specs, check_vma=False)
```

```python
import jax
import jax.numpy as jnp
from jax import lax
from jax.experimental.layout import Layout, with_layout_constraint
from jax.sharding import Mesh
from jax.sharding import PartitionSpec as P

ROW = ("x", "y")
NEAR = ("pair", "core")
Z = ("parity", "pair")
COL = (*Z, "core")
SWAP = [(0, 1), (1, 0)]
CROSSED = [[0, 3], [1, 2]]


def exchanged(blocks, axis):
    return lax.all_to_all(blocks, axis, split_axis=0, concat_axis=0, tiled=True)


def from_everyone(array, axis):
    return exchanged(jnp.broadcast_to(array, (lax.axis_size(axis), *array.shape)), axis)


def taken_together(array, axis):
    return jnp.sum(from_everyone(array, axis), axis=0)


def my_sum(array, axis):
    count = lax.axis_size(axis)
    blocks = array.reshape(count, array.shape[0] // count, *array.shape[1:])
    return jnp.sum(exchanged(blocks, axis), axis=0)


def product(left, right, precision=lax.Precision.HIGHEST):
    return jnp.dot(left, right, precision=precision, preferred_element_type=jnp.float32)


def part_of(array, start, rows):
    return lax.dynamic_slice(array, (start, 0), (rows, array.shape[1]), allow_negative_indices=False)


def local(rhs, factor, inverses):
    span_rows = inverses.shape[2]
    span_cols = factor.shape[1] // 2
    first_rhs = rhs[:span_rows]
    second_rhs = rhs[span_rows : 2 * span_rows]
    spots = lax.axis_size(Z)
    rows = (rhs.shape[0] - 2 * span_rows) // (2 * spots)
    half = spots * rows
    side = lax.axis_index("core") ^ lax.axis_index("pair")
    pair = lax.axis_index("pair")
    quarter = half // 2
    place = 2 * span_rows + side * half + lax.axis_index(Z) * rows
    near_rows = span_rows // 2
    near = lax.axis_index("core") * near_rows
    starts = (side * half, (1 - side) * half, pair * quarter, (1 - pair) * quarter, near, place)
    first_part = product(inverses[0], first_rhs)
    first_part, second_rhs, starts = lax.optimization_barrier((first_part, second_rhs, starts))
    half_kept, half_sent, quarter_kept, quarter_sent, near, place = starts

    first_sol = taken_together(first_part, ROW)
    coupled = lax.optimization_barrier(product(factor[:span_rows, :span_cols], first_sol))
    coupled = with_layout_constraint(coupled, Layout((0, 1)))
    coupled = lax.all_gather(coupled, NEAR, axis=0)
    coupled = lax.dynamic_slice(
        coupled, (0, near, 0), (coupled.shape[0], near_rows, coupled.shape[2]), allow_negative_indices=False
    )
    coupled = taken_together(jnp.sum(coupled, axis=0), "parity")
    coupled = lax.all_gather(coupled, "core", axis=0, tiled=True)
    second_sol = taken_together(product(inverses[1], second_rhs - coupled), ROW)

    both = lax.optimization_barrier(jnp.concatenate([first_sol, second_sol], 0))
    terms = with_layout_constraint(product(factor[span_rows:], both, lax.Precision.HIGH), Layout((0, 1)))
    terms = terms.reshape(2, spots // 2, 2, rows, -1).swapaxes(1, 2).reshape(2 * half, -1)
    sent, kept = part_of(terms, half_sent, half), part_of(terms, half_kept, half)
    sent, kept, rhs = lax.optimization_barrier((sent, kept, rhs))
    taken = lax.ppermute(sent, "core", SWAP)
    trailing = part_of(rhs, place, rows)
    taken, trailing = lax.optimization_barrier((taken, trailing))
    terms = kept + taken
    sent, kept = part_of(terms, quarter_sent, quarter), part_of(terms, quarter_kept, quarter)
    sent = lax.all_gather(sent, NEAR, axis=0, tiled=True, axis_index_groups=CROSSED)
    taken = part_of(sent, quarter_sent, quarter)
    terms = my_sum(kept + taken, "parity")

    rings = [[2 * z + (z + start) % 2 for z in range(spots)] for start in range(2)]
    mine = lax.all_gather(trailing - terms, COL, axis=0, tiled=True, axis_index_groups=rings)
    other = lax.ppermute(mine, "core", SWAP)
    remaining = jnp.where(
        side == 0, jnp.concatenate([mine, other], 0), jnp.concatenate([other, mine], 0)
    )
    return (both, remaining)


def solution(mesh):
    rows, cols = mesh.devices.shape
    shape = (4, rows // 4, cols // 4, 2, 2)
    torus = Mesh(mesh.devices.reshape(shape), (*ROW, *COL))
    in_specs = (P(ROW, None), P(ROW, COL), P(None, COL, ROW))
    out_specs = (P(COL, None), P(ROW, None))
    return jax.shard_map(local, mesh=torus, in_specs=in_specs, out_specs=out_specs, check_vma=False)
```

```python
import jax
import jax.numpy as jnp
from jax import lax
from jax.experimental.layout import Layout, with_layout_constraint
from jax.sharding import Mesh
from jax.sharding import PartitionSpec as P

ROW = ("x", "y")
NEAR = ("pair", "core")
Z = ("parity", "pair")
COL = (*Z, "core")
SWAP = [(0, 1), (1, 0)]
CROSSED = [[0, 3], [1, 2]]


def exchanged(blocks, axis):
    return lax.all_to_all(blocks, axis, split_axis=0, concat_axis=0, tiled=True)


def from_everyone(array, axis):
    return exchanged(jnp.broadcast_to(array, (lax.axis_size(axis), *array.shape)), axis)


def taken_together(array, axis):
    return jnp.sum(from_everyone(array, axis), axis=0)


def my_sum(array, axis):
    count = lax.axis_size(axis)
    blocks = array.reshape(count, array.shape[0] // count, *array.shape[1:])
    return jnp.sum(exchanged(blocks, axis), axis=0)


def product(left, right, precision=lax.Precision.HIGHEST):
    return jnp.dot(left, right, precision=precision, preferred_element_type=jnp.float32)


def part_of(array, start, rows):
    return lax.dynamic_slice(array, (start, 0), (rows, array.shape[1]), allow_negative_indices=False)


def local(rhs, factor, inverses):
    span_rows = inverses.shape[2]
    span_cols = factor.shape[1] // 2
    first_rhs = rhs[:span_rows]
    second_rhs = rhs[span_rows : 2 * span_rows]
    spots = lax.axis_size(Z)
    rows = (rhs.shape[0] - 2 * span_rows) // (2 * spots)
    half = spots * rows
    side = lax.axis_index("core") ^ lax.axis_index("pair")
    pair = lax.axis_index("pair")
    quarter = half // 2
    place = 2 * span_rows + side * half + lax.axis_index(Z) * rows
    near_rows = span_rows // lax.axis_size(NEAR)
    near = lax.axis_index(NEAR) * near_rows
    kept_at, sent_at = span_rows + side * half, span_rows + (1 - side) * half
    theirs_at = (1 - lax.axis_index("core")) * 2 * (factor.shape[1] // 2)
    starts = (kept_at, sent_at, pair * quarter, (1 - pair) * quarter, near, place, theirs_at)
    first_part = product(inverses[0], first_rhs)
    first_part, second_rhs, starts = lax.optimization_barrier((first_part, second_rhs, starts))
    half_kept, half_sent, quarter_kept, quarter_sent, near, place, theirs_at = starts

    first_sol = taken_together(first_part, ROW)
    coupled = lax.optimization_barrier(product(factor[:span_rows, :span_cols], first_sol))
    coupled = with_layout_constraint(coupled, Layout((0, 1)))
    coupled = lax.all_gather(coupled, NEAR, axis=0)
    coupled = lax.dynamic_slice(
        coupled, (0, near, 0), (coupled.shape[0], near_rows, coupled.shape[2]), allow_negative_indices=False
    )
    coupled = jnp.sum(coupled, axis=0)
    coupled = lax.all_gather(taken_together(coupled, "parity"), NEAR, axis=0, tiled=True)
    second_part = product(inverses[1], second_rhs - coupled)
    second_part, factor, rhs = lax.optimization_barrier((second_part, factor, rhs))
    sent, kept = part_of(factor, half_sent, half), part_of(factor, half_kept, half)
    came = lax.ppermute(sent, "core", SWAP)
    trailing = part_of(rhs, place, rows)
    second_sol = taken_together(second_part, ROW)
    second_sol, kept, trailing = lax.optimization_barrier((second_sol, kept, trailing))

    both = lax.optimization_barrier(jnp.concatenate([first_sol, second_sol], 0))
    all_both = lax.all_gather(both, "core", axis=0, tiled=True)
    theirs = part_of(all_both, theirs_at, both.shape[0])
    terms = product(kept, both, lax.Precision.HIGH) + product(came, theirs, lax.Precision.HIGH)
    terms = with_layout_constraint(terms, Layout((0, 1)))
    terms = terms.reshape(spots // 2, 2, rows, -1).swapaxes(0, 1).reshape(half, -1)
    sent, kept = part_of(terms, quarter_sent, quarter), part_of(terms, quarter_kept, quarter)
    sent = lax.all_gather(sent, NEAR, axis=0, tiled=True, axis_index_groups=CROSSED)
    taken = part_of(sent, quarter_sent, quarter)
    terms = my_sum(kept + taken, "parity")

    rings = [[2 * z + (z + start) % 2 for z in range(spots)] for start in range(2)]
    mine = lax.all_gather(trailing - terms, COL, axis=0, tiled=True, axis_index_groups=rings)
    other = lax.ppermute(mine, "core", SWAP)
    remaining = jnp.where(
        side == 0, jnp.concatenate([mine, other], 0), jnp.concatenate([other, mine], 0)
    )
    return (both, remaining)


def solution(mesh):
    rows, cols = mesh.devices.shape
    shape = (4, rows // 4, cols // 4, 2, 2)
    torus = Mesh(mesh.devices.reshape(shape), (*ROW, *COL))
    in_specs = (P(ROW, None), P(ROW, COL), P(None, COL, ROW))
    out_specs = (P(COL, None), P(ROW, None))
    return jax.shard_map(local, mesh=torus, in_specs=in_specs, out_specs=out_specs, check_vma=False)
```

```python
import jax
import jax.numpy as jnp
from jax import lax
from jax.experimental.layout import Layout, with_layout_constraint
from jax.sharding import Mesh
from jax.sharding import PartitionSpec as P

ROW = ("x", "y")
NEAR = ("pair", "core")
Z = ("parity", "pair")
COL = (*Z, "core")
SWAP = [(0, 1), (1, 0)]


def exchanged(blocks, axis):
    return lax.all_to_all(blocks, axis, split_axis=0, concat_axis=0, tiled=True)


def from_everyone(array, axis):
    return exchanged(jnp.broadcast_to(array, (lax.axis_size(axis), *array.shape)), axis)


def taken_together(array, axis):
    return jnp.sum(from_everyone(array, axis), axis=0)


def my_sum(array, axis):
    count = lax.axis_size(axis)
    blocks = array.reshape(count, array.shape[0] // count, *array.shape[1:])
    return jnp.sum(exchanged(blocks, axis), axis=0)


def product(left, right, precision=lax.Precision.HIGHEST):
    return jnp.dot(left, right, precision=precision, preferred_element_type=jnp.float32)


def part_of(array, start, rows):
    return lax.dynamic_slice(array, (start, 0), (rows, array.shape[1]), allow_negative_indices=False)


def quarter_of(blocks, first, pair):
    sizes = (blocks.shape[0] // 2, 1, *blocks.shape[2:])
    part = lax.dynamic_slice(blocks, (first, pair, 0, 0), sizes, allow_negative_indices=False)
    return part.reshape(-1, blocks.shape[-1])


def local(rhs, factor, inverses):
    span_rows = inverses.shape[2]
    span_cols = factor.shape[1] // 2
    first_rhs = rhs[:span_rows]
    second_rhs = rhs[span_rows : 2 * span_rows]
    spots = lax.axis_size(Z)
    rows = (rhs.shape[0] - 2 * span_rows) // (2 * spots)
    half = spots * rows
    side = lax.axis_index("core") ^ lax.axis_index("pair")
    pair = lax.axis_index("pair")
    place = 2 * span_rows + side * half + lax.axis_index(Z) * rows
    near_rows = span_rows // lax.axis_size(NEAR)
    near = lax.axis_index(NEAR) * near_rows
    core, other_core = lax.axis_index("core"), 1 - lax.axis_index("core")
    other_pair, group = 1 - pair, spots // 2
    unknowns = factor.shape[1]
    starts = (
        1 + side * group,
        1 + (1 - side) * group,
        pair,
        other_pair,
        near,
        place,
        (pair * 2 + other_core) * unknowns,
        (other_pair * 2 + other_core) * unknowns,
        (other_pair * 2 + core) * unknowns,
    )
    first_part = product(inverses[0], first_rhs)
    first_part, second_rhs, starts = lax.optimization_barrier((first_part, second_rhs, starts))
    blocks_at, other_at, pair, other_pair, near, place, across_at, crossed_at, straight_at = starts

    first_sol = taken_together(first_part, ROW)
    coupled = lax.optimization_barrier(product(factor[:span_rows, :span_cols], first_sol))
    coupled = with_layout_constraint(coupled, Layout((0, 1)))
    coupled = lax.all_gather(coupled, NEAR, axis=0)
    coupled = lax.dynamic_slice(
        coupled, (0, near, 0), (coupled.shape[0], near_rows, coupled.shape[2]), allow_negative_indices=False
    )
    coupled = jnp.sum(coupled, axis=0)
    coupled = lax.all_gather(taken_together(coupled, "parity"), NEAR, axis=0, tiled=True)
    second_part = product(inverses[1], second_rhs - coupled)
    second_part, factor, rhs = lax.optimization_barrier((second_part, factor, rhs))
    blocks = factor.reshape(-1, 2, rows, factor.shape[1])
    own = quarter_of(blocks, blocks_at, pair)
    across = quarter_of(blocks, other_at, pair)
    crossed = quarter_of(blocks, blocks_at, other_pair)
    straight = quarter_of(blocks, other_at, other_pair)
    across = lax.ppermute(across, NEAR, [(0, 1), (1, 0), (2, 3), (3, 2)])
    crossed = lax.ppermute(crossed, NEAR, [(0, 3), (3, 0), (1, 2), (2, 1)])
    straight = lax.ppermute(straight, NEAR, [(0, 2), (2, 0), (1, 3), (3, 1)])
    trailing = part_of(rhs, place, rows)
    second_sol = taken_together(second_part, ROW)
    second_sol, own, trailing = lax.optimization_barrier((second_sol, own, trailing))

    both = lax.optimization_barrier(jnp.concatenate([first_sol, second_sol], 0))
    near_both = lax.all_gather(both, NEAR, axis=0, tiled=True)
    terms = product(own, both, lax.Precision.HIGH)
    for part, at in ((across, across_at), (crossed, crossed_at), (straight, straight_at)):
        terms = terms + product(part, part_of(near_both, at, both.shape[0]), lax.Precision.HIGH)
    terms = my_sum(with_layout_constraint(terms, Layout((0, 1))), "parity")

    rings = [[2 * z + (z + start) % 2 for z in range(spots)] for start in range(2)]
    mine = lax.all_gather(trailing - terms, COL, axis=0, tiled=True, axis_index_groups=rings)
    other = lax.ppermute(mine, "core", SWAP)
    remaining = jnp.where(
        side == 0, jnp.concatenate([mine, other], 0), jnp.concatenate([other, mine], 0)
    )
    return (both, remaining)


def solution(mesh):
    rows, cols = mesh.devices.shape
    shape = (4, rows // 4, cols // 4, 2, 2)
    torus = Mesh(mesh.devices.reshape(shape), (*ROW, *COL))
    in_specs = (P(ROW, None), P(ROW, COL), P(None, COL, ROW))
    out_specs = (P(COL, None), P(ROW, None))
    return jax.shard_map(local, mesh=torus, in_specs=in_specs, out_specs=out_specs, check_vma=False)
```

```python
import jax
import jax.numpy as jnp
from jax import lax
from jax.experimental.layout import Layout, with_layout_constraint
from jax.sharding import Mesh
from jax.sharding import PartitionSpec as P

ROW = ("x", "y")
NEAR = ("pair", "core")
Z = ("parity", "pair")
COL = (*Z, "core")
SWAP = [(0, 1), (1, 0)]


def exchanged(blocks, axis):
    return lax.all_to_all(blocks, axis, split_axis=0, concat_axis=0, tiled=True)


def from_everyone(array, axis):
    return exchanged(jnp.broadcast_to(array, (lax.axis_size(axis), *array.shape)), axis)


def taken_together(array, axis):
    return jnp.sum(from_everyone(array, axis), axis=0)


def my_sum(array, axis):
    count = lax.axis_size(axis)
    blocks = array.reshape(count, array.shape[0] // count, *array.shape[1:])
    return jnp.sum(exchanged(blocks, axis), axis=0)


def product(left, right, precision=lax.Precision.HIGHEST):
    return jnp.dot(left, right, precision=precision, preferred_element_type=jnp.float32)


def part_of(array, start, rows):
    return lax.dynamic_slice(array, (start, 0), (rows, array.shape[1]), allow_negative_indices=False)


def quarter_of(blocks, first, pair):
    sizes = (blocks.shape[0] // 2, 1, *blocks.shape[2:])
    part = lax.dynamic_slice(blocks, (first, pair, 0, 0), sizes, allow_negative_indices=False)
    return part.reshape(-1, blocks.shape[-1])


def local(rhs, factor, inverses):
    span_rows = inverses.shape[2]
    span_cols = factor.shape[1] // 2
    first_rhs = rhs[:span_rows]
    second_rhs = rhs[span_rows : 2 * span_rows]
    spots = lax.axis_size(Z)
    rows = (rhs.shape[0] - 2 * span_rows) // (2 * spots)
    half = spots * rows
    side = lax.axis_index("core") ^ lax.axis_index("pair")
    pair = lax.axis_index("pair")
    place = 2 * span_rows + side * half + lax.axis_index(Z) * rows
    near_rows = span_rows // lax.axis_size(NEAR)
    near = lax.axis_index(NEAR) * near_rows
    core, other_core = lax.axis_index("core"), 1 - lax.axis_index("core")
    other_pair, group = 1 - pair, spots // 2
    unknowns = factor.shape[1]
    starts = (
        1 + side * group,
        1 + (1 - side) * group,
        pair,
        other_pair,
        near,
        place,
        (pair * 2 + other_core) * unknowns,
        (other_pair * 2 + other_core) * unknowns,
        (other_pair * 2 + core) * unknowns,
    )
    first_part = product(inverses[0], first_rhs)
    first_part, second_rhs, starts = lax.optimization_barrier((first_part, second_rhs, starts))
    blocks_at, other_at, pair, other_pair, near, place, across_at, crossed_at, straight_at = starts

    first_sol = taken_together(first_part, ROW)
    coupled = lax.optimization_barrier(product(factor[:span_rows, :span_cols], first_sol))
    coupled = with_layout_constraint(coupled, Layout((0, 1)))
    coupled = lax.all_gather(coupled, NEAR, axis=0)
    coupled = lax.dynamic_slice(
        coupled, (0, near, 0), (coupled.shape[0], near_rows, coupled.shape[2]), allow_negative_indices=False
    )
    coupled = jnp.sum(coupled, axis=0)
    coupled = lax.all_gather(taken_together(coupled, "parity"), NEAR, axis=0, tiled=True)
    second_part = product(inverses[1], second_rhs - coupled)
    second_part, factor, rhs = lax.optimization_barrier((second_part, factor, rhs))
    blocks = factor.reshape(-1, 2, rows, factor.shape[1])
    own = quarter_of(blocks, blocks_at, pair)
    across = quarter_of(blocks, other_at, pair)
    crossed = quarter_of(blocks, blocks_at, other_pair)
    straight = quarter_of(blocks, other_at, other_pair)
    across = lax.ppermute(across, NEAR, [(0, 1), (1, 0), (2, 3), (3, 2)])
    crossed = lax.ppermute(crossed, NEAR, [(0, 3), (3, 0), (1, 2), (2, 1)])
    straight = lax.ppermute(straight, NEAR, [(0, 2), (2, 0), (1, 3), (3, 1)])
    trailing = part_of(rhs, place, rows)
    second_sol = taken_together(second_part, ROW)
    second_sol, own, trailing = lax.optimization_barrier((second_sol, own, trailing))

    both = lax.optimization_barrier(jnp.concatenate([first_sol, second_sol], 0))
    near_both = lax.all_gather(both, NEAR, axis=0, tiled=True)
    theirs = [part_of(near_both, at, both.shape[0]) for at in (across_at, crossed_at, straight_at)]
    columns = jnp.concatenate([own, across, crossed, straight], 1)
    terms = product(columns, jnp.concatenate([both, *theirs], 0), lax.Precision.HIGH)
    terms = my_sum(with_layout_constraint(terms, Layout((0, 1))), "parity")

    rings = [[2 * z + (z + start) % 2 for z in range(spots)] for start in range(2)]
    mine = lax.all_gather(trailing - terms, COL, axis=0, tiled=True, axis_index_groups=rings)
    other = lax.ppermute(mine, "core", SWAP)
    remaining = jnp.where(
        side == 0, jnp.concatenate([mine, other], 0), jnp.concatenate([other, mine], 0)
    )
    return (both, remaining)


def solution(mesh):
    rows, cols = mesh.devices.shape
    shape = (4, rows // 4, cols // 4, 2, 2)
    torus = Mesh(mesh.devices.reshape(shape), (*ROW, *COL))
    in_specs = (P(ROW, None), P(ROW, COL), P(None, COL, ROW))
    out_specs = (P(COL, None), P(ROW, None))
    return jax.shard_map(local, mesh=torus, in_specs=in_specs, out_specs=out_specs, check_vma=False)
```
